32 devices in a mesh: row: 16 (over z, y, x), col: 2 (over core).
Axes of the slice: x: 2, y: 2, z: 4, core: 2. Of those that a mesh axis runs over, the one named last changes fastest.
Arguments:
- tokens: bfloat16 [8192, 6144], P('row', 'col'), may hold values from -6 to 6
- w_blocks: bfloat16 [96, 81920], P('col', 'row'), may hold values from -0.25 to 0.25
- hidden_bias: bfloat16 [12288], P('col'), may hold values from -3 to 3
- pattern: int32 [96, 5], replicated, may hold values from 0 to 47, as said below
- grad_act: bfloat16 [8192, 12288], P('row', 'col'), may hold values from -6 to 6
Outputs:
- activation: bfloat16 [8192, 12288], P('row', 'col')
- weight_grad: float32 [96, 81920], P('col', 'row')
- bias_grad: float32 [12288], P('col')
The draws below stay inside these ranges and needn't reach their ends.
Inputs may be any that keep to these rules, and one draw needn't show every extreme that they name: `pattern`: panel p holds input blocks p * 24 to (p + 1) * 24 - 1, and hidden block h lies in group g = h // 48. Slot 0 of h names a block in panel g; slot k for 1 <= k <= 3 names a block in panel (g + 2^(k-1)) mod 2; slot 4 names one of the blocks 0 to 1. Names may repeat within a hidden block.
All inputs are finite; a program needn't handle non-finite values.
Results may differ from the reference program's by a relative error of at most 0.003.
Values may be sent and summed in bfloat16 or wider, within the bound.
A program may use at most 192 MiB of HBM per device.

```python
import math
import jax
import jax.numpy as jnp
from jax import lax

D = 6144
FF = 12288
BLK = 128
LEVELS = 3
GLOB = 2
KSLOT = 5
DB = 48
HB = 96
GROUPS = 2
PANEL = 24
HBC = 48
TOKENS = 8192


def draw_pattern(key, part):
    hidden_ids = jnp.arange(HB, dtype=jnp.int32)
    group_ids = hidden_ids // HBC
    subkeys = jax.random.split(key, LEVELS + 2)
    columns = []
    for slot_index in range(LEVELS + 1):
        offset = 0 if slot_index == 0 else 2 ** (slot_index - 1)
        home_panel = (group_ids + offset) % GROUPS
        picks = jax.random.randint(subkeys[slot_index], (HB,), 0, PANEL, dtype=jnp.int32)
        columns.append(home_panel * PANEL + picks)
    columns.append(jax.random.randint(subkeys[LEVELS + 1], (HB,), 0, GLOB, dtype=jnp.int32))
    pattern = jnp.stack(columns, axis=1)
    pattern = pattern.at[HB - 1, 0].set(DB - 1)
    return pattern


def steps_of(key, extent, cuts, least, largest):
    loudness = 1.0
    for axis_at, parts in cuts:
        draws = jax.random.uniform(jax.random.fold_in(jax.random.fold_in(key, 6), axis_at), (parts,), jnp.float32, least / len(cuts), largest / len(cuts))
        loudness = loudness * jnp.repeat(jnp.exp(draws), extent[axis_at] // parts).reshape((-1,) + (1,) * (len(extent) - 1 - axis_at))
    return loudness


def scatter_about(stream_key, dims, deviation, reach, cuts=(), kind=jnp.bfloat16):
    level = steps_of(stream_key, dims, cuts, -0.22, 0.18) if cuts else 1.0
    values = jax.random.normal(stream_key, dims, jnp.float32) * deviation * level
    return jnp.minimum(jnp.maximum(values, -reach), reach).astype(kind)


def setup_inputs(seed: int = 0) -> dict:
    key_list = jax.random.split(jax.random.key(seed), 6)
    return {
        "tokens": scatter_about(key_list[0], (TOKENS, D), 1.0, 6.0, ((0, 16), (1, 2))),
        "w_blocks": scatter_about(key_list[1], (HB, KSLOT * BLK * BLK), (KSLOT * BLK) ** -0.5, 0.25, ((0, 2), (1, 16))),
        "hidden_bias": scatter_about(key_list[2], (FF,), 0.5, 3.0, ((0, 2),)),
        "pattern": draw_pattern(jax.random.fold_in(key_list[5], 71), 0),
        "grad_act": scatter_about(key_list[4], (TOKENS, FF), 1.0, 6.0, ((0, 16), (1, 2))),
    }


def reference(tokens, w_blocks, hidden_bias, pattern, grad_act):
    tok_count = tokens.shape[0]
    tok_blocks = tokens.reshape(tok_count, DB, BLK)
    inv_scale = 1.0 / math.sqrt(tok_count)

    def per_block(block_index):
        slot_ids = pattern[block_index]
        selected = jnp.take(tok_blocks, slot_ids, axis=1).reshape(tok_count, KSLOT * BLK).astype(jnp.float32)
        block_weight = w_blocks[block_index].reshape(KSLOT * BLK, BLK).astype(jnp.float32)
        bias_piece = lax.dynamic_slice_in_dim(hidden_bias, block_index * BLK, BLK).astype(jnp.float32)
        pre_act = jnp.dot(selected, block_weight, preferred_element_type=jnp.float32) + bias_piece
        act_value, pull_back = jax.vjp(jax.nn.gelu, pre_act)
        grad_piece = lax.dynamic_slice_in_dim(grad_act, block_index * BLK, BLK, 1).astype(jnp.float32)
        grad_pre = pull_back(grad_piece)[0]
        grad_rounded = lax.optimization_barrier(grad_pre.astype(jnp.bfloat16)).astype(jnp.float32)
        weight_piece = jnp.dot(selected.T, grad_rounded, preferred_element_type=jnp.float32) * inv_scale
        bias_piece_grad = lax.optimization_barrier(jnp.sum(grad_pre, axis=0)) * inv_scale
        return (act_value.astype(jnp.bfloat16), weight_piece.reshape(-1), bias_piece_grad)
    acts, weight_grad, bias_parts = lax.map(per_block, jnp.arange(HB, dtype=jnp.int32))
    activation = jnp.transpose(acts, (1, 0, 2)).reshape(tok_count, HB * BLK)
    return (activation, weight_grad, bias_parts.reshape(HB * BLK))
```

```python
import functools
import math

import jax
import jax.numpy as jnp
from jax import lax
from jax.experimental import pallas as pl
from jax.experimental.pallas import tpu as pltpu
from jax.sharding import PartitionSpec as P

BLK = 128
LEVELS = 3
GLOB = 2
KSLOT = 5
MESH = pl.DeviceIdType.MESH
VMEM_LIMIT = 60 * 1024 * 1024


def from_behind(block, axis, distance):
    devices = range(lax.axis_size(axis))
    route = [((i - distance) % len(devices), i) for i in devices]
    return lax.ppermute(block, axis, route)


def broadcast(value, axis, source):
    kept = jnp.where(lax.axis_index(axis) == source, value, 0).astype(value.dtype)
    return lax.psum(kept, axis)


def plain_body(tokens, w_blocks, hidden_bias, pattern, grad_act):
    tok_rows = tokens.shape[0]
    local_blocks = w_blocks.shape[0]
    col_count = lax.axis_size("col")
    col_index = lax.axis_index("col")
    panel_blocks = tokens.shape[1] // BLK
    inv_scale = 1.0 / math.sqrt(tok_rows * lax.axis_size("row"))
    gathered_weights = lax.all_gather(w_blocks, "row", axis=1, tiled=True)
    weights = gathered_weights.reshape(local_blocks, KSLOT, BLK, BLK)
    my_pattern = lax.dynamic_slice_in_dim(pattern, col_index * local_blocks, local_blocks, 0)
    own_panel = tokens.reshape(tok_rows, panel_blocks, BLK)
    pieces = [jnp.take(own_panel, my_pattern[:, 0] - col_index * panel_blocks, axis=1)]
    for level_index in range(LEVELS):
        offset = 2**level_index % col_count
        if offset == 0:
            source = own_panel
        else:
            moved = from_behind(tokens, "col", -offset)
            source = moved.reshape(tok_rows, panel_blocks, BLK)
        home_panel = (col_index + offset) % col_count
        pieces.append(
            jnp.take(source, my_pattern[:, level_index + 1] - home_panel * panel_blocks, axis=1)
        )
    shared = broadcast(tokens[:, : GLOB * BLK], "col", 0).reshape(tok_rows, GLOB, BLK)
    pieces.append(jnp.take(shared, my_pattern[:, LEVELS + 1], axis=1))
    picked = jnp.stack(pieces, axis=2)
    pre_act = jnp.einsum("thkc,hkcd->thd", picked, weights, preferred_element_type=jnp.float32)
    pre_act = pre_act + hidden_bias.astype(jnp.float32).reshape(local_blocks, BLK)
    act_value, pull_back = jax.vjp(jax.nn.gelu, pre_act)
    activation = act_value.reshape(tok_rows, local_blocks * BLK).astype(jnp.bfloat16)
    grad_pre = pull_back(grad_act.astype(jnp.float32).reshape(tok_rows, local_blocks, BLK))[0]
    grad_rounded = grad_pre.astype(jnp.bfloat16)
    weight_terms = (
        jnp.einsum("thkc,thd->hkcd", picked, grad_rounded, preferred_element_type=jnp.float32)
        * inv_scale
    )
    weight_terms = weight_terms.reshape(local_blocks, KSLOT * BLK * BLK)
    weight_grad = lax.psum_scatter(weight_terms, "row", scatter_dimension=1, tiled=True)
    bias_terms = jnp.sum(grad_pre, axis=0).reshape(local_blocks * BLK) * inv_scale
    bias_grad = lax.psum(bias_terms, "row")
    return (activation, weight_grad, bias_grad)


def fused_kernel(quads, chunks, blk_rows, scale, hop,
                 pat_ref, tok_ref, w_ref, bias_ref, grad_ref,
                 act_ref, out_ref, bout_ref,
                 table, wbuf, part, psend, arecv, zout, zrecv, bsend, brecv,
                 b_ref, bx, by, by_out, bz, bz_out,
                 tl_s, t_s, t_r, lw_s, gb_s, gb_r, gz_s, gz_r, ga_s, ga_r,
                 ra_s, ra_r, rz_s, rz_r, rb_s, rb_r, b_s, b_r):
    step = pl.program_id(0)
    n = wbuf.shape[2]
    pairs = chunks * n // (2 * blk_rows)
    span = 2 * pairs // chunks
    rows = quads * 4
    row = lax.axis_index("row")
    col = lax.axis_index("col")
    z, y, x = row // 4, (row // 2) % 2, row % 2
    x_row = z * 4 + y * 2 + 1 - x
    y_row = z * 4 + (1 - y) * 2 + x
    panel = tok_ref.shape[1] // BLK
    begin = first_block(quads, hop)
    last = begin + 2 * pairs

    def link(src, dst, s, r, target):
        return pltpu.make_async_remote_copy(
            src_ref=src, dst_ref=dst, send_sem=s, recv_sem=r,
            device_id=(target, col), device_id_type=MESH
        )

    def local_token(i):
        return pltpu.make_async_copy(
            tok_ref.at[:, pl.ds(i * BLK, BLK)], table.at[col * panel + i], tl_s)

    def far_token(i):
        return pltpu.make_async_remote_copy(
            src_ref=tok_ref.at[:, pl.ds(i * BLK, BLK)], dst_ref=table.at[col * panel + i],
            send_sem=t_s, recv_sem=t_r, device_id=(row, 1 - col), device_id_type=MESH)

    def sides(c):
        k = c % 2
        a = y + k * (x - y)
        b = x + k * (y - x)
        return a, b, y_row + k * (x_row - y_row), x_row + k * (y_row - x_row)

    def pair_at(side, plane):
        return pl.ds((side * quads + plane) * 2, 2)

    def spot(side, plane, b):
        return (side * quads + plane) * 2 + b

    def load_weight(c):
        a, b, _, _ = sides(c)
        return pltpu.make_async_copy(w_ref.at[c], wbuf.at[c, spot(a, z, b)], lw_s.at[c])

    def gather_near(c):
        a, b, _, b_row = sides(c)
        here = wbuf.at[c, spot(a, z, b)]
        return link(here, here, gb_s, gb_r.at[c], b_row)

    def gather_z(c, plane, up):
        a, _, _, _ = sides(c)
        here = wbuf.at[c, pair_at(a, plane)]
        return link(here, here, gz_s.at[c, up, plane], gz_r.at[c, plane], row + (8 * up - 4))

    def gather_far(c, plane):
        a, _, a_row, _ = sides(c)
        here = wbuf.at[c, pair_at(a, plane)]
        return link(here, here, ga_s, ga_r.at[c, plane], a_row)

    def scatter_far(c, plane):
        _, _, a_row, _ = sides(c)
        return link(psend.at[c, pl.ds(plane * 2, 2)], arecv.at[c, pl.ds(plane * 2, 2)],
                    ra_s, ra_r.at[c, plane], a_row)

    def scatter_z(c, plane, up, slot):
        return link(zout.at[c, pl.ds(plane * 2, 2)], zrecv.at[c, pl.ds(slot * 2, 2)],
                    rz_s.at[c, plane], rz_r.at[c, slot], row + (8 * up - 4))

    def scatter_near(c):
        _, _, _, b_row = sides(c)
        return link(bsend.at[c], brecv.at[c], rb_s, rb_r.at[c], b_row)

    def gather_hop(c, i):
        if i == 0:
            gather_near(c).wait_recv()
            pl.when(z < quads - 1)(lambda: gather_z(c, z, 1).start())
            pl.when(z > 0)(lambda: gather_z(c, z, 0).start())
            gather_far(c, z).start()
            return

        @pl.when(z - i >= 0)
        def _():
            gather_z(c, z - i, 1).wait_recv()
            pl.when(z < quads - 1)(lambda: gather_z(c, z - i, 1).start())
            gather_far(c, z - i).start()

        @pl.when(z + i < quads)
        def _():
            gather_z(c, z + i, 0).wait_recv()
            pl.when(z > 0)(lambda: gather_z(c, z + i, 0).start())
            gather_far(c, z + i).start()

    def scatter_first(c):
        a, _, _, _ = sides(c)

        def go(plane):
            psend[c, pl.ds(plane * 2, 2)] = part[c, pair_at(1 - a, plane)].astype(jnp.bfloat16)
            scatter_far(c, plane).start()

        for i in reversed(range(1, quads)):
            pl.when(z + i < quads)(lambda i=i: go(z + i))
            pl.when(z - i >= 0)(lambda i=i: go(z - i))
        go(z)

    def scatter_hop(c, i):
        a, b, _, _ = sides(c)

        def pass_on(plane, up, chained):
            scatter_far(c, plane).wait_recv()
            mine = part[c, pair_at(a, plane)] + arecv[c, pl.ds(plane * 2, 2)].astype(jnp.float32)

            @pl.when(chained)
            def _():
                scatter_z(c, plane, up, plane).wait_recv()
                zout[c, pl.ds(plane * 2, 2)] = (
                    mine + zrecv[c, pl.ds(plane * 2, 2)].astype(jnp.float32)).astype(jnp.bfloat16)

            @pl.when(jnp.logical_not(chained))
            def _():
                zout[c, pl.ds(plane * 2, 2)] = mine.astype(jnp.bfloat16)

            slot = quads if up == 0 and i == 1 else plane
            scatter_z(c, plane, up, slot).start()

        if i > 0:
            pl.when(z + i < quads)(lambda: pass_on(z + i, 1, z > 0))
            pl.when(z - i >= 0)(lambda: pass_on(z - i, 0, z < quads - 1))
            return
        scatter_far(c, z).wait_recv()
        own = pair_at(a, z)
        part[c, own] = part[c, own] + arecv[c, pl.ds(z * 2, 2)].astype(jnp.float32)

        @pl.when(z > 0)
        def _():
            scatter_z(c, z, 1, z).wait_recv()
            part[c, own] = part[c, own] + zrecv[c, pl.ds(z * 2, 2)].astype(jnp.float32)

        @pl.when(z < quads - 1)
        def _():
            scatter_z(c, z, 0, quads).wait_recv()
            part[c, own] = part[c, own] + zrecv[c, pl.ds(quads * 2, 2)].astype(jnp.float32)

        bsend[c] = part[c, spot(a, z, 1 - b)].astype(jnp.bfloat16)
        scatter_near(c).start()

    def scatter_last(c):
        a, b, _, _ = sides(c)
        scatter_near(c).wait_recv()
        total = part[c, spot(a, z, b)] + brecv[c].astype(jnp.float32)
        out_ref[pl.ds(pl.multiple_of(c * n, n), n), :] = total * scale

    def gathered(c):
        for plane in range(quads):
            gather_far(c, plane).wait_recv()

    def compute(block, j):
        c = block // span
        base = (col * 2 * pairs + block) * KSLOT
        skip = j * blk_rows // 16 * 16
        tall = -(-(j * blk_rows - skip + blk_rows) // 16) * 16
        cut = slice(j * blk_rows - skip, j * blk_rows - skip + blk_rows)
        inner = (block % span) // 2 * (2 * blk_rows)
        at = pl.multiple_of(inner + skip, 16)
        k = c % 2
        spots = []
        for r in range(rows):
            q, v, u = r // 4, (r // 2) % 2, r % 2
            spots.append(spot(v + k * (u - v), q, u + k * (v - u)))
        w = [wbuf[c, s, pl.ds(at, tall), :].astype(jnp.float32)[cut] for s in spots]
        w = jnp.concatenate(w, axis=0).astype(jnp.bfloat16)
        piece = pl.ds(j * BLK, BLK)
        picks = [table[pat_ref[base + s]] for s in range(KSLOT)]
        sel = jnp.concatenate(picks, axis=1)
        v = jnp.dot(sel, w, preferred_element_type=jnp.float32)
        v = v + bias_ref[:, piece].astype(jnp.float32)
        e = math.sqrt(2.0 / math.pi)
        sq = v * v
        t = jnp.tanh(v * (e + (e * 0.044715) * sq))
        lift = 0.5 + 0.5 * t
        act_ref[:, piece] = (v * lift).astype(jnp.bfloat16)
        slope = lift + (0.5 * v) * (1.0 - t * t) * (e + (3.0 * 0.044715 * e) * sq)
        grad = grad_ref[:, piece].astype(jnp.float32) * slope
        b_ref[pl.ds(block, 1), :] = jnp.sum(grad, axis=0, keepdims=True) * scale
        out = lax.dot_general(sel, grad.astype(jnp.bfloat16), (((0,), (0,)), ((), ())),
                              preferred_element_type=jnp.float32)
        put = pl.ds(pl.multiple_of(inner + j * blk_rows, 8), blk_rows)
        for r in range(rows):
            part[c, spots[r], put, :] = out[r * blk_rows:(r + 1) * blk_rows]

    def swap(src, dst, i, target):
        return link(src, dst, b_s.at[i], b_r.at[i], target)

    def other(d):
        return (z + d) % quads * 4 + y * 2 + x

    @pl.when(step == 0)
    def _():
        for c in range(chunks):
            load_weight(c).start()
        for i in range(panel):
            local_token(i).start()
        barrier = pltpu.get_barrier_semaphore()
        peers = [(x_row, col), (y_row, col), (row, 1 - col)]
        peers += [(other(d), col) for d in range(1, quads)]
        for peer in peers:
            pl.semaphore_signal(barrier, inc=1, device_id=peer, device_id_type=MESH)
        pl.semaphore_wait(barrier, len(peers))
        for i in range(panel):
            far_token(i).start()

    def bias_moves(i):
        if i == 0:
            swap(b_ref, bx, 0, x_row).start()
        elif i == 1:
            swap(b_ref, bx, 0, x_row).wait()
            by_out[...] = b_ref[...] + bx[...]
            swap(by_out, by, 1, y_row).start()
        elif i == 2:
            swap(by_out, by, 1, y_row).wait()
            bz_out[...] = by_out[...] + by[...]
            for d in range(1, quads):
                swap(bz_out, bz.at[d - 1], d + 1, other(d)).start()
        else:
            total = bz_out[...]
            for d in range(1, quads):
                swap(bz_out, bz.at[d - 1], d + 1, other(d)).wait()
                total += bz[d - 1]
            bout_ref[...] = total

    for j in range(2):
        now = 2 * step + j

        def on(offset, do, *more):
            if offset % 2 != j:
                return
            m = now - offset

            @pl.when((m >= 0) & (m < span * chunks) & (m % span == 0))
            def _():
                do(m // span, *more)

        for i in reversed(range(quads)):
            on(hop * (i + 1), gather_hop, i)

        def own(c):
            load_weight(c).wait()
            gather_near(c).start()

        on(0, own)
        if begin % 2 == j:
            @pl.when(now == begin)
            def _():
                here = table.at[pl.ds(col * panel, panel)]
                pltpu.make_async_copy(here, here, tl_s).wait()
                come = table.at[pl.ds((1 - col) * panel, panel)]
                pltpu.make_async_copy(come, come, t_r).wait()

        on(begin + span + hop * (quads + 1), scatter_last)
        for i in range(quads):
            on(begin + span + hop * (quads - i), scatter_hop, i)
        on(begin + span, scatter_first)
        for i in range(4):
            if (last + i * hop) % 2 == j:
                pl.when(now == last + i * hop)(functools.partial(bias_moves, i))
        on(begin, gathered)

        @pl.when((now >= begin) & (now < last))
        def _():
            compute(now - begin, j)

    @pl.when(step == pl.num_programs(0) - 1)
    def _():
        mine = table.at[pl.ds(col * panel, panel)]
        pltpu.make_async_copy(mine, mine, t_s).wait()
        link(brecv, brecv, gb_s, gb_r.at[0], x_row).wait_send()
        link(arecv, arecv, ga_s, ga_r.at[0, 0], x_row).wait_send()
        link(psend, psend, ra_s, ra_r.at[0, 0], x_row).wait_send()
        link(bsend, bsend, rb_s, rb_r.at[0], x_row).wait_send()

        @pl.loop(0, chunks)
        def _(c):
            for plane in range(quads):
                pl.when((z < quads - 1) & (plane <= z))(
                    lambda plane=plane: gather_z(c, plane, 1).wait_send())
                pl.when((z > 0) & (plane >= z))(
                    lambda plane=plane: gather_z(c, plane, 0).wait_send())
                pl.when(plane != z)(
                    lambda plane=plane: scatter_z(c, plane, 1, plane).wait_send())


def first_block(quads, hop):
    return (hop * (quads + 1) + 1) // 2 * 2


def fused(pat, tokens, weights, bias, grad_act, quads, scale):
    tok, hidden = grad_act.shape
    blocks = hidden // BLK
    pairs = blocks // 2
    total_rows = weights.shape[0]
    blk_rows = total_rows // blocks
    chunks = next(c for c in (12, 8, 6, 4, 3, 2, 1) if pairs % c == 0)
    n = total_rows // chunks
    hop = 3
    rows = quads * 4
    begin = first_block(quads, hop)
    span = blocks // chunks
    steps = (begin + blocks + hop * (quads + 1)) // 2 + 1
    at = lambda i: jnp.minimum(jnp.maximum(i - begin // 2, 0), pairs - 1)
    wide = lambda m: pl.BlockSpec((m, 2 * BLK), lambda i, p: (0, at(i)))
    fixed = lambda *s: pl.BlockSpec(s, lambda i, p: (0, 0))
    any_spec = pl.BlockSpec(memory_space=pl.ANY)
    dma = pltpu.SemaphoreType.DMA
    bf = lambda *s: pltpu.VMEM(s, jnp.bfloat16)
    f32 = lambda *s: pltpu.VMEM(s, jnp.float32)
    b = (blocks, BLK)
    return pl.pallas_call(
        functools.partial(fused_kernel, quads, chunks, blk_rows, scale, hop),
        out_shape=(
            jax.ShapeDtypeStruct((tok, hidden), jnp.bfloat16),
            jax.ShapeDtypeStruct((total_rows, BLK), jnp.float32),
            jax.ShapeDtypeStruct(b, jnp.float32),
        ),
        grid_spec=pltpu.PrefetchScalarGridSpec(
            num_scalar_prefetch=1, grid=(steps,),
            in_specs=[any_spec, any_spec, wide(1), wide(tok)],
            out_specs=[wide(tok), fixed(total_rows, BLK), fixed(*b)],
            scratch_shapes=[
                bf(2 * tokens.shape[1] // BLK, tok, BLK), bf(chunks, rows, n, BLK),
                f32(chunks, rows, n, BLK), bf(chunks, 2 * quads, n, BLK),
                bf(chunks, 2 * quads, n, BLK), bf(chunks, 2 * quads, n, BLK),
                bf(chunks, 2 * quads + 2, n, BLK), bf(chunks, n, BLK), bf(chunks, n, BLK),
                f32(*b), f32(*b), f32(*b), f32(*b), f32(quads - 1, *b), f32(*b),
                dma, dma, dma, dma((chunks,)), dma, dma((chunks,)),
                dma((chunks, 2, quads)), dma((chunks, quads)), dma, dma((chunks, quads)),
                dma, dma((chunks, quads)), dma((chunks, quads)), dma((chunks, quads + 1)),
                dma, dma((chunks,)), dma((quads + 1,)), dma((quads + 1,)),
            ],
        ),
        compiler_params=pltpu.CompilerParams(collective_id=0, has_side_effects=True,
                                             vmem_limit_bytes=VMEM_LIMIT),
    )(pat, tokens, weights.reshape(chunks, n, BLK), bias, grad_act)


def kernel_body(tokens, w_blocks, hidden_bias, pattern, grad_act):
    tok_rows = tokens.shape[0]
    local_blocks, width = w_blocks.shape
    rows = lax.axis_size("row")
    scale = 1.0 / math.sqrt(tok_rows * rows)
    flat = w_blocks.reshape(local_blocks * width // BLK, BLK)
    activation, weight_grad, bias_grad = fused(
        pattern.reshape(-1), tokens, flat, hidden_bias.reshape(1, -1), grad_act, rows // 4, scale)
    return activation, weight_grad.reshape(local_blocks, width), bias_grad.reshape(-1)


def body(tokens, w_blocks, hidden_bias, pattern, grad_act):
    rows = lax.axis_size("row")
    piece = w_blocks.shape[1] // BLK
    fits = lax.axis_size("col") == 2 and rows % 4 == 0 and rows > 4
    fits = fits and piece % 8 == 0 and w_blocks.shape[0] % 8 == 0
    run = kernel_body if fits else plain_body
    return run(tokens, w_blocks, hidden_bias, pattern, grad_act)


def solution(mesh):
    return jax.shard_map(
        body,
        mesh=mesh,
        in_specs=(P("row", "col"), P("col", "row"), P("col"), P(), P("row", "col")),
        out_specs=(P("row", "col"), P("col", "row"), P("col")),
        check_vma=False,
    )
```

```python
import functools
import math

import jax
import jax.numpy as jnp
from jax import lax
from jax.experimental import pallas as pl
from jax.experimental.pallas import tpu as pltpu
from jax.sharding import PartitionSpec as P

BLK = 128
LEVELS = 3
GLOB = 2
KSLOT = 5
MESH = pl.DeviceIdType.MESH
VMEM_LIMIT = 50 * 1024 * 1024


def from_behind(block, axis, distance):
    devices = range(lax.axis_size(axis))
    route = [((i - distance) % len(devices), i) for i in devices]
    return lax.ppermute(block, axis, route)


def broadcast(value, axis, source):
    kept = jnp.where(lax.axis_index(axis) == source, value, 0).astype(value.dtype)
    return lax.psum(kept, axis)


def plain_body(tokens, w_blocks, hidden_bias, pattern, grad_act):
    tok_rows = tokens.shape[0]
    local_blocks = w_blocks.shape[0]
    col_count = lax.axis_size("col")
    col_index = lax.axis_index("col")
    panel_blocks = tokens.shape[1] // BLK
    inv_scale = 1.0 / math.sqrt(tok_rows * lax.axis_size("row"))
    gathered_weights = lax.all_gather(w_blocks, "row", axis=1, tiled=True)
    weights = gathered_weights.reshape(local_blocks, KSLOT, BLK, BLK)
    my_pattern = lax.dynamic_slice_in_dim(pattern, col_index * local_blocks, local_blocks, 0)
    own_panel = tokens.reshape(tok_rows, panel_blocks, BLK)
    pieces = [jnp.take(own_panel, my_pattern[:, 0] - col_index * panel_blocks, axis=1)]
    for level_index in range(LEVELS):
        offset = 2**level_index % col_count
        if offset == 0:
            source = own_panel
        else:
            moved = from_behind(tokens, "col", -offset)
            source = moved.reshape(tok_rows, panel_blocks, BLK)
        home_panel = (col_index + offset) % col_count
        pieces.append(
            jnp.take(source, my_pattern[:, level_index + 1] - home_panel * panel_blocks, axis=1)
        )
    shared = broadcast(tokens[:, : GLOB * BLK], "col", 0).reshape(tok_rows, GLOB, BLK)
    pieces.append(jnp.take(shared, my_pattern[:, LEVELS + 1], axis=1))
    picked = jnp.stack(pieces, axis=2)
    pre_act = jnp.einsum("thkc,hkcd->thd", picked, weights, preferred_element_type=jnp.float32)
    pre_act = pre_act + hidden_bias.astype(jnp.float32).reshape(local_blocks, BLK)
    act_value, pull_back = jax.vjp(jax.nn.gelu, pre_act)
    activation = act_value.reshape(tok_rows, local_blocks * BLK).astype(jnp.bfloat16)
    grad_pre = pull_back(grad_act.astype(jnp.float32).reshape(tok_rows, local_blocks, BLK))[0]
    grad_rounded = grad_pre.astype(jnp.bfloat16)
    weight_terms = (
        jnp.einsum("thkc,thd->hkcd", picked, grad_rounded, preferred_element_type=jnp.float32)
        * inv_scale
    )
    weight_terms = weight_terms.reshape(local_blocks, KSLOT * BLK * BLK)
    weight_grad = lax.psum_scatter(weight_terms, "row", scatter_dimension=1, tiled=True)
    bias_terms = jnp.sum(grad_pre, axis=0).reshape(local_blocks * BLK) * inv_scale
    bias_grad = lax.psum(bias_terms, "row")
    return (activation, weight_grad, bias_grad)


def fused_kernel(quads, chunks, blk_rows, scale, plan,
                 pat_ref, tok_ref, w_ref, bias_ref, grad_ref,
                 act_ref, out_ref, bout_ref,
                 table, wbuf, part, psend, arecv, zout, zrecv, bsend, brecv,
                 lines, shift, b_ref, bx, by, by_out, bz, bz_out,
                 tl_s, t_s, t_r, gb_s, gb_r, gz_s, gz_r, ga_s, ga_r,
                 ra_s, ra_r, rz_s, rz_r, rb_s, rb_r, b_s, b_r):
    step = pl.program_id(0)
    n = wbuf.shape[2]
    pairs = chunks * n // (2 * blk_rows)
    span = 2 * pairs // chunks
    rows = quads * 4
    row = lax.axis_index("row")
    col = lax.axis_index("col")
    z, y, x = row // 4, (row // 2) % 2, row % 2
    x_row = z * 4 + y * 2 + 1 - x
    y_row = z * 4 + (1 - y) * 2 + x
    panel = tok_ref.shape[1] // BLK
    gather_at, begin, scatter_at = plan
    last = begin + 2 * pairs
    after = begin + span

    def link(src, dst, s, r, target):
        return pltpu.make_async_remote_copy(
            src_ref=src, dst_ref=dst, send_sem=s, recv_sem=r,
            device_id=(target, col), device_id_type=MESH
        )

    def local_token(i):
        return pltpu.make_async_copy(
            tok_ref.at[:, pl.ds(i * BLK, BLK)], table.at[col * panel + i], tl_s)

    def far_token(i):
        return pltpu.make_async_remote_copy(
            src_ref=tok_ref.at[:, pl.ds(i * BLK, BLK)], dst_ref=table.at[col * panel + i],
            send_sem=t_s, recv_sem=t_r, device_id=(row, 1 - col), device_id_type=MESH)

    def sides(c):
        k = c % 2
        a = y + k * (x - y)
        b = x + k * (y - x)
        return a, b, y_row + k * (x_row - y_row), x_row + k * (y_row - x_row)

    def pair_at(side, plane):
        return pl.ds((side * quads + plane) * 2, 2)

    def spot(side, plane, b):
        return (side * quads + plane) * 2 + b

    def gather_near(c):
        a, b, _, b_row = sides(c)
        here = wbuf.at[c, spot(a, z, b)]
        return link(here, here, gb_s, gb_r.at[c], b_row)

    def gather_z(c, plane, up):
        a, _, _, _ = sides(c)
        here = wbuf.at[c, pair_at(a, plane)]
        return link(here, here, gz_s.at[c, up, plane], gz_r.at[c, plane], row + (8 * up - 4))

    def gather_far(c, plane):
        a, _, a_row, _ = sides(c)
        here = wbuf.at[c, pair_at(a, plane)]
        return link(here, here, ga_s, ga_r.at[c, plane], a_row)

    def scatter_far(c, plane):
        _, _, a_row, _ = sides(c)
        return link(psend.at[c, pl.ds(plane * 2, 2)], arecv.at[c, pl.ds(plane * 2, 2)],
                    ra_s, ra_r.at[c, plane], a_row)

    def scatter_z(c, plane, up, slot):
        return link(zout.at[c, pl.ds(plane * 2, 2)], zrecv.at[c, pl.ds(slot * 2, 2)],
                    rz_s.at[c, plane], rz_r.at[c, slot], row + (8 * up - 4))

    def scatter_near(c):
        _, _, _, b_row = sides(c)
        return link(bsend.at[c], brecv.at[c], rb_s, rb_r.at[c], b_row)

    def gather_hop(c, i):
        if i == 0:
            gather_near(c).wait_recv()
            pl.when(z < quads - 1)(lambda: gather_z(c, z, 1).start())
            pl.when(z > 0)(lambda: gather_z(c, z, 0).start())
            gather_far(c, z).start()
            return

        @pl.when(z - i >= 0)
        def _():
            gather_z(c, z - i, 1).wait_recv()
            pl.when(z < quads - 1)(lambda: gather_z(c, z - i, 1).start())
            gather_far(c, z - i).start()

        @pl.when(z + i < quads)
        def _():
            gather_z(c, z + i, 0).wait_recv()
            pl.when(z > 0)(lambda: gather_z(c, z + i, 0).start())
            gather_far(c, z + i).start()

    def scatter_first(c):
        a, _, _, _ = sides(c)

        def go(plane):
            psend[c, pl.ds(plane * 2, 2)] = part[c, pair_at(1 - a, plane)].astype(jnp.bfloat16)
            scatter_far(c, plane).start()

        for i in reversed(range(1, quads)):
            pl.when(z + i < quads)(lambda i=i: go(z + i))
            pl.when(z - i >= 0)(lambda i=i: go(z - i))
        go(z)

    def scatter_hop(c, i):
        a, b, _, _ = sides(c)

        def pass_on(plane, up, chained):
            scatter_far(c, plane).wait_recv()
            mine = part[c, pair_at(a, plane)] + arecv[c, pl.ds(plane * 2, 2)].astype(jnp.float32)

            @pl.when(chained)
            def _():
                scatter_z(c, plane, up, plane).wait_recv()
                zout[c, pl.ds(plane * 2, 2)] = (
                    mine + zrecv[c, pl.ds(plane * 2, 2)].astype(jnp.float32)).astype(jnp.bfloat16)

            @pl.when(jnp.logical_not(chained))
            def _():
                zout[c, pl.ds(plane * 2, 2)] = mine.astype(jnp.bfloat16)

            slot = quads if up == 0 and i == 1 else plane
            scatter_z(c, plane, up, slot).start()

        if i > 0:
            pl.when(z + i < quads)(lambda: pass_on(z + i, 1, z > 0))
            pl.when(z - i >= 0)(lambda: pass_on(z - i, 0, z < quads - 1))
            return
        scatter_far(c, z).wait_recv()
        own = pair_at(a, z)
        part[c, own] = part[c, own] + arecv[c, pl.ds(z * 2, 2)].astype(jnp.float32)

        @pl.when(z > 0)
        def _():
            scatter_z(c, z, 1, z).wait_recv()
            part[c, own] = part[c, own] + zrecv[c, pl.ds(z * 2, 2)].astype(jnp.float32)

        @pl.when(z < quads - 1)
        def _():
            scatter_z(c, z, 0, quads).wait_recv()
            part[c, own] = part[c, own] + zrecv[c, pl.ds(quads * 2, 2)].astype(jnp.float32)

        bsend[c] = part[c, spot(a, z, 1 - b)].astype(jnp.bfloat16)
        scatter_near(c).start()

    def scatter_last(c):
        a, b, _, _ = sides(c)
        scatter_near(c).wait_recv()
        total = part[c, spot(a, z, b)] + brecv[c].astype(jnp.float32)
        out_ref[pl.ds(pl.multiple_of(c * n, n), n), :] = total * scale

    def gathered(c):
        for plane in range(quads):
            gather_far(c, plane).wait_recv()

    def compute(block, j):
        c = block // span
        base = col * 2 * pairs + block
        skip = j * blk_rows // 16 * 16
        tall = -(-(j * blk_rows - skip + blk_rows) // 16) * 16
        cut = slice(j * blk_rows - skip, j * blk_rows - skip + blk_rows)
        inner = (block % span) // 2 * (2 * blk_rows)
        at = pl.multiple_of(inner + skip, 16)
        k = c % 2
        spots = []
        for r in range(rows):
            q, v, u = r // 4, (r // 2) % 2, r % 2
            spots.append(spot(v + k * (u - v), q, u + k * (v - u)))
        w = [wbuf[c, s, pl.ds(at, tall), :].astype(jnp.float32)[cut] for s in spots]
        w = jnp.concatenate(w, axis=0).astype(jnp.bfloat16)
        piece = pl.ds(j * BLK, BLK)
        picks = [table[pat_ref[s, base]] for s in range(KSLOT)]
        sel = jnp.concatenate(picks, axis=1)
        v = jnp.dot(sel, w, preferred_element_type=jnp.float32)
        v = v + shift[pl.ds(block, 1), :]
        e = math.sqrt(2.0 / math.pi)
        sq = v * v
        t = jnp.tanh(v * (e + (e * 0.044715) * sq))
        lift = 0.5 + 0.5 * t
        act_ref[:, piece] = (v * lift).astype(jnp.bfloat16)
        slope = lift + (0.5 * v) * (1.0 - t * t) * (e + (3.0 * 0.044715 * e) * sq)
        grad = grad_ref[:, piece].astype(jnp.float32) * slope
        b_ref[pl.ds(block, 1), :] = jnp.sum(grad, axis=0, keepdims=True) * scale
        out = lax.dot_general(sel, grad.astype(jnp.bfloat16), (((0,), (0,)), ((), ())),
                              preferred_element_type=jnp.float32)
        put = pl.ds(pl.multiple_of(inner + j * blk_rows, 8), blk_rows)
        for r in range(rows):
            part[c, spots[r], put, :] = out[r * blk_rows:(r + 1) * blk_rows]

    def swap(src, dst, i, target):
        return link(src, dst, b_s.at[i], b_r.at[i], target)

    def other(d):
        return (z + d) % quads * 4 + y * 2 + x

    @pl.when(step == 0)
    def _():
        for i in range(panel):
            local_token(i).start()
        wide = w_ref.shape[1] // BLK
        for i in range(wide):
            lines[pl.ds(i, 2 * pairs, stride=wide), :] = (
                w_ref[:, i * BLK:(i + 1) * BLK].astype(jnp.float32))
        for c in range(chunks):
            a, b, _, _ = sides(c)
            wbuf[c, spot(a, z, b)] = lines[c * n:(c + 1) * n, :].astype(jnp.bfloat16)
        shift[...] = bias_ref[...].astype(jnp.float32).reshape(2 * pairs, BLK)
        barrier = pltpu.get_barrier_semaphore()
        peers = [(x_row, col), (y_row, col), (row, 1 - col)]
        peers += [(other(d), col) for d in range(1, quads)]
        for peer in peers:
            pl.semaphore_signal(barrier, inc=1, device_id=peer, device_id_type=MESH)
        pl.semaphore_wait(barrier, len(peers))
        for i in range(panel):
            far_token(i).start()

    def bias_moves(i):
        if i == 0:
            swap(b_ref, bx, 0, x_row).start()
        elif i == 1:
            swap(b_ref, bx, 0, x_row).wait()
            by_out[...] = b_ref[...] + bx[...]
            swap(by_out, by, 1, y_row).start()
        elif i == 2:
            swap(by_out, by, 1, y_row).wait()
            bz_out[...] = by_out[...] + by[...]
            for d in range(1, quads):
                swap(bz_out, bz.at[d - 1], d + 1, other(d)).start()
        else:
            total = bz_out[...]
            for d in range(1, quads):
                swap(bz_out, bz.at[d - 1], d + 1, other(d)).wait()
                total += bz[d - 1]
            bout_ref[...] = total

    def own(c):
        gather_near(c).start()

    @pl.when(step == 0)
    def _():
        for c in range(min(chunks, -(gather_at[0] // span))):
            own(c)

    for j in range(2):
        now = 2 * step + j

        def on(offset, do, *more):
            if offset % 2 != j:
                return
            m = now - offset

            @pl.when((m >= 0) & (m < span * chunks) & (m % span == 0))
            def _():
                do(m // span, *more)

        for i in reversed(range(quads)):
            on(gather_at[i + 1], gather_hop, i)
        on(gather_at[0], own)
        if begin % 2 == j:
            @pl.when(now == begin)
            def _():
                here = table.at[pl.ds(col * panel, panel)]
                pltpu.make_async_copy(here, here, tl_s).wait()
                come = table.at[pl.ds((1 - col) * panel, panel)]
                pltpu.make_async_copy(come, come, t_r).wait()

        on(after + scatter_at[quads + 1], scatter_last)
        for i in range(quads):
            on(after + scatter_at[quads - i], scatter_hop, i)
        on(after + scatter_at[0], scatter_first)
        for i in range(4):
            if (last + 3 * i) % 2 == j:
                pl.when(now == last + 3 * i)(functools.partial(bias_moves, i))
        on(begin, gathered)

        @pl.when((now >= begin) & (now < last))
        def _():
            compute(now - begin, j)

    @pl.when(step == pl.num_programs(0) - 1)
    def _():
        mine = table.at[pl.ds(col * panel, panel)]
        pltpu.make_async_copy(mine, mine, t_s).wait()
        link(brecv, brecv, gb_s, gb_r.at[0], x_row).wait_send()
        link(arecv, arecv, ga_s, ga_r.at[0, 0], x_row).wait_send()
        link(psend, psend, ra_s, ra_r.at[0, 0], x_row).wait_send()
        link(bsend, bsend, rb_s, rb_r.at[0], x_row).wait_send()

        @pl.loop(0, chunks)
        def _(c):
            for plane in range(quads):
                pl.when((z < quads - 1) & (plane <= z))(
                    lambda plane=plane: gather_z(c, plane, 1).wait_send())
                pl.when((z > 0) & (plane >= z))(
                    lambda plane=plane: gather_z(c, plane, 0).wait_send())
                pl.when(plane != z)(
                    lambda plane=plane: scatter_z(c, plane, 1, plane).wait_send())


def plan_of(quads):
    if quads == 4:
        return (-27, 5, 12, 15, 18), 20, (0, 3, 4, 8, 15, 21)
    gather_at = tuple(3 * i for i in range(quads + 1))
    return gather_at, 4 * quads, tuple(3 * i for i in range(quads + 2))


def fused(pat, tokens, weights, bias, grad_act, quads, scale):
    tok, hidden = grad_act.shape
    blocks = hidden // BLK
    pairs = blocks // 2
    total_rows = weights.size // BLK
    blk_rows = total_rows // blocks
    chunks = next(c for c in (24, 12, 8, 6, 4, 3, 2, 1) if pairs % c == 0)
    n = total_rows // chunks
    plan = plan_of(quads)
    rows = quads * 4
    begin = plan[1]
    span = blocks // chunks
    steps = (begin + blocks + max(plan[2][-1], 9)) // 2 + 1
    at = lambda i: jnp.minimum(jnp.maximum(i - begin // 2, 0), pairs - 1)
    wide = lambda m: pl.BlockSpec((m, 2 * BLK), lambda i, p: (0, at(i)))
    fixed = lambda *s: pl.BlockSpec(s, lambda i, p: (0, 0))
    any_spec = pl.BlockSpec(memory_space=pl.ANY)
    vmem = pl.BlockSpec(memory_space=pltpu.VMEM)
    dma = pltpu.SemaphoreType.DMA
    bf = lambda *s: pltpu.VMEM(s, jnp.bfloat16)
    f32 = lambda *s: pltpu.VMEM(s, jnp.float32)
    b = (blocks, BLK)
    return pl.pallas_call(
        functools.partial(fused_kernel, quads, chunks, blk_rows, scale, plan),
        out_shape=(
            pltpu.VMEM((tok, hidden), jnp.bfloat16),
            pltpu.VMEM((total_rows, BLK), jnp.float32),
            pltpu.VMEM(b, jnp.float32),
        ),
        grid_spec=pltpu.PrefetchScalarGridSpec(
            num_scalar_prefetch=1, grid=(steps,),
            in_specs=[any_spec, vmem, vmem, wide(tok)],
            out_specs=[wide(tok), fixed(total_rows, BLK), fixed(*b)],
            scratch_shapes=[
                bf(2 * tokens.shape[1] // BLK, tok, BLK), bf(chunks, rows, n, BLK),
                f32(chunks, rows, n, BLK), bf(chunks, 2 * quads, n, BLK),
                bf(chunks, 2 * quads, n, BLK), bf(chunks, 2 * quads, n, BLK),
                bf(chunks, 2 * quads + 2, n, BLK), bf(chunks, n, BLK), bf(chunks, n, BLK),
                f32(total_rows, BLK), f32(*b), f32(*b), f32(*b), f32(*b), f32(*b), f32(quads - 1, *b), f32(*b),
                dma, dma, dma, dma, dma((chunks,)),
                dma((chunks, 2, quads)), dma((chunks, quads)), dma, dma((chunks, quads)),
                dma, dma((chunks, quads)), dma((chunks, quads)), dma((chunks, quads + 1)),
                dma, dma((chunks,)), dma((quads + 1,)), dma((quads + 1,)),
            ],
        ),
        compiler_params=pltpu.CompilerParams(collective_id=0, has_side_effects=True,
                                             vmem_limit_bytes=VMEM_LIMIT),
    )(pat, tokens, weights, bias, grad_act)


def finish_kernel(parts, act_in, grad_in, bias_in, act_out, grad_out, bias_out, sems):
    tall = act_in.shape[0] // parts
    copies = [pltpu.make_async_copy(bias_in, bias_out, sems.at[parts])]
    copies[0].start()
    for i in range(parts):
        cut = pl.ds(i * tall, tall)
        copies.append(pltpu.make_async_copy(act_in.at[cut], act_out.at[cut], sems.at[i]))
        copies[-1].start()
    blocks, width = grad_out.shape
    each = width // BLK
    for i in range(each):
        grad_out[:, i * BLK:(i + 1) * BLK] = grad_in[pl.ds(i, blocks, stride=each), :]
    for copy in copies:
        copy.wait()


def finish(act, grad, bias, blocks):
    parts = 4
    any_spec = pl.BlockSpec(memory_space=pl.ANY)
    vmem = pl.BlockSpec(memory_space=pltpu.VMEM)
    return pl.pallas_call(
        functools.partial(finish_kernel, parts),
        out_shape=(
            jax.ShapeDtypeStruct(act.shape, act.dtype),
            jax.ShapeDtypeStruct((blocks, grad.size // blocks), grad.dtype),
            jax.ShapeDtypeStruct(bias.shape, bias.dtype),
        ),
        in_specs=[any_spec, vmem, any_spec],
        out_specs=(any_spec, vmem, any_spec),
        scratch_shapes=[pltpu.SemaphoreType.DMA((parts + 1,))],
        compiler_params=pltpu.CompilerParams(vmem_limit_bytes=8 * 1024 * 1024),
    )(act, grad, bias)


def kernel_body(tokens, w_blocks, hidden_bias, pattern, grad_act):
    tok_rows = tokens.shape[0]
    local_blocks = w_blocks.shape[0]
    rows = lax.axis_size("row")
    scale = 1.0 / math.sqrt(tok_rows * rows)
    activation, weight_grad, bias_grad = fused(
        pattern.T, tokens, w_blocks, hidden_bias, grad_act, rows // 4, scale)
    activation, weight_grad, bias_grad = finish(activation, weight_grad, bias_grad, local_blocks)
    return activation, weight_grad, bias_grad.reshape(-1)


def body(tokens, w_blocks, hidden_bias, pattern, grad_act):
    rows = lax.axis_size("row")
    piece = w_blocks.shape[1] // BLK
    fits = lax.axis_size("col") == 2 and rows % 4 == 0 and rows > 4
    fits = fits and piece % 8 == 0 and w_blocks.shape[0] % 8 == 0
    run = kernel_body if fits else plain_body
    return run(tokens, w_blocks, hidden_bias, pattern, grad_act)


def solution(mesh):
    return jax.shard_map(
        body,
        mesh=mesh,
        in_specs=(P("row", "col"), P("col", "row"), P("col"), P(), P("row", "col")),
        out_specs=(P("row", "col"), P("col", "row"), P("col")),
        check_vma=False,
    )
```
